32 devices in a mesh: tm: 8 (over y, x, core), vocab: 4 (over z).
Axes of the slice: x: 2, y: 2, z: 4, core: 2. Of those that a mesh axis runs over, the one named last changes fastest.
Arguments:
- drift_noise: bfloat16 [64, 128, 8192], P('tm', None, 'vocab'), may hold values from -6 to 6
- counts: bfloat16 [64, 128, 8192], P('tm', None, 'vocab'), may hold values from 0 to 12, as said below
- base_logits: float32 [128, 8192], P(None, 'vocab'), may hold values from -8 to 300
- drift_scale: float32 [128], replicated, may hold values from 0.05 to 0.5
Outputs:
- grad_noise: bfloat16 [64, 128, 8192], P('tm', None, 'vocab')
- grad_base: float32 [128, 8192], P('tm', 'vocab')
The draws below stay inside these ranges and needn't reach their ends.
Inputs may be any that keep to these rules, and one draw needn't show every extreme that they name: `counts`: whole numbers.
All inputs are finite; a program needn't handle non-finite values.
Results may differ from the reference program's by a relative error of at most 0.003.
Values sent between devices are 32-bit elements; how exact they have to be, the bound alone decides.
A program may use at most 128 MiB of HBM per device.

```python
import math
import jax
import jax.numpy as jnp
from jax import lax

TOPICS = 128
VOCAB = 8192
SLICES = 64


def draw_counts(key, part):
    column = jnp.arange(VOCAB, dtype=jnp.int32)
    highest = 12 - 10 * column // VOCAB
    raw = jax.random.randint(key, (SLICES, TOPICS, VOCAB), 0, 1 << 20, dtype=jnp.int32)
    values = raw % (highest + 1)
    return values.astype(jnp.float32).astype(jnp.bfloat16)


def draw_base_logits(key, part):
    column = jnp.arange(VOCAB, dtype=jnp.int32)
    trend = 1.5 - 3.0 * column.astype(jnp.float32) / VOCAB
    rough = jax.random.normal(key, (TOPICS, VOCAB), jnp.float32)
    return jnp.clip(rough, -6.0, 6.0) + trend[None, :]


def steps_of(own_key, extent, split, smallest, top_value):
    loudness = 1.0
    for dim, blocks in split:
        heights = jax.random.uniform(jax.random.fold_in(jax.random.fold_in(own_key, 6), dim), (blocks,), jnp.float32, smallest / len(split), top_value / len(split))
        loudness = loudness * jnp.repeat(jnp.exp(heights), extent[dim] // blocks).reshape((-1,) + (1,) * (len(extent) - 1 - dim))
    return loudness


def scatter_about(key, shape, width, most, cuts=(), kind=jnp.bfloat16):
    entries = jax.random.normal(key, shape, jnp.float32) * width
    if len(cuts) > 0:
        entries = steps_of(key, shape, cuts, -0.22, 0.18) * entries
    return jnp.clip(entries, min=-most, max=most).astype(kind)


def setup_inputs(seed: int = 0) -> dict:
    streams_of = jax.random.split(jax.random.key(seed), 5)
    drift_noise = scatter_about(streams_of[0], (SLICES, TOPICS, VOCAB), 1.0, 6.0, ((0, 8), (2, 4)))
    counts = draw_counts(jax.random.fold_in(streams_of[4], 71), 0)
    base_logits = draw_base_logits(jax.random.fold_in(streams_of[4], 71), 0)
    drift_scale = jnp.clip(jnp.exp(jax.random.uniform(streams_of[3], (TOPICS,), jnp.float32, math.log(0.05), math.log(0.5))), 0.05, 0.5)
    return dict(drift_noise=drift_noise, counts=counts, base_logits=base_logits, drift_scale=drift_scale)


def reference(drift_noise, counts, base_logits, drift_scale):
    spread = drift_scale[:, None]

    def forward(carry, inputs):
        noise, count_row = inputs
        carry = carry + spread * noise.astype(jnp.float32)
        logits = base_logits + carry
        top = jnp.max(logits, axis=1, keepdims=True)
        expo = jnp.exp(logits - top)
        total = jnp.sum(expo, axis=1, keepdims=True)
        count_f = count_row.astype(jnp.float32)
        tokens = jnp.sum(count_f, axis=1, keepdims=True)
        slope = count_f - tokens * (expo / total)
        return carry, slope

    start = jnp.zeros(base_logits.shape, jnp.float32)
    _, slopes = lax.scan(forward, start, (drift_noise, counts))

    def backward(carry, slope):
        carry = carry + slope
        return carry, carry

    whole, suffix = lax.scan(backward, start, slopes, reverse=True)
    grad_noise = (spread[None] * suffix - drift_noise.astype(jnp.float32)).astype(jnp.bfloat16)
    return grad_noise, whole
```

```python
import functools

import jax
import jax.numpy as jnp
from jax import lax
from jax.experimental import pallas as pl
from jax.experimental.pallas import tpu as pltpu
from jax.sharding import PartitionSpec as P

MESH = pl.DeviceIdType.MESH
KC = 16
HB = KC // 2
LANE = 128


def kernel(n, nz, nb, rows, out_rows, dims,
           noise_hbm, counts_hbm, base_hbm, scale_ref, gn_hbm, gb_hbm,
           noise, counts, base, spread, work, out, query, ratio, stat, stat_in, tot, tot_out,
           own, mate, src, got, acc,
           in_sem, out_sem, gb_sem, mate_s, mate_r, hop_s, hop_r, acc_s, acc_r, stat_s, stat_r, tot_s, tot_r):
    T, K, V = dims
    NC = K // KC
    LB = min(256, V)
    me = lax.axis_index("tm")
    z = lax.axis_index("vocab")
    core = lax.rem(me, 2)
    partner = me + 1 - 2 * core

    def bit(j):
        return lax.rem(me // (2 ** j), 2)

    def across(j):
        return me + (1 - 2 * bit(j)) * (2 ** j)

    def krows(c):
        return pl.ds(pl.multiple_of(c * KC, KC), KC)

    def load_noise(c):
        return pltpu.make_async_copy(noise_hbm.at[:, krows(c), :], noise.at[c], in_sem.at[0, c])

    def load_counts(c):
        return pltpu.make_async_copy(counts_hbm.at[:, krows(c), :], counts.at[c], in_sem.at[1, c])

    def load_base(c):
        return pltpu.make_async_copy(base_hbm.at[krows(c), :], base.at[c], in_sem.at[2, c])

    def store_out(c):
        return pltpu.make_async_copy(out.at[c], gn_hbm.at[:, krows(c), :], out_sem.at[c])

    def send(a, b, s, r, device):
        return pltpu.make_async_remote_copy(src_ref=a, dst_ref=b, send_sem=s, recv_sem=r,
                                            device_id=device, device_id_type=MESH)

    def mate_copy(p, c):
        return send(own.at[p, c], mate.at[p, c], mate_s.at[p, c], mate_r.at[p, c], {"tm": partner})

    def hop_copy(p, j, c):
        return send(src.at[p, j, c], got.at[p, j, c], hop_s.at[p, j, c], hop_r.at[p, j, c],
                    {"tm": across(j + 1)})

    def acc_copy(p, c):
        return send(acc.at[p, c, core], acc.at[p, c, core], acc_s.at[p, c], acc_r.at[p, c], {"tm": partner})

    def stat_copy(d, c):
        return send(stat.at[c], stat_in.at[d - 1, c], stat_s.at[d - 1, c], stat_r.at[d - 1, c],
                    {"vocab": lax.rem(z + d, nz)})

    def tot_copy():
        return send(tot_out, tot.at[core], tot_s.at[0], tot_r.at[0], {"tm": partner})

    def start_loads(c, _):
        load_noise(c).start()
        load_base(c).start()
        return 0

    lax.fori_loop(0, NC, start_loads, 0)
    lax.fori_loop(0, NC, lambda c, _: (load_counts(c).start(), 0)[1], 0)

    barrier = pltpu.get_barrier_semaphore()
    for j in range(nb + 1):
        pl.semaphore_signal(barrier, inc=1, device_id={"tm": across(j)}, device_id_type=MESH)
    for d in range(1, nz):
        pl.semaphore_signal(barrier, inc=1, device_id={"vocab": lax.rem(z + d, nz)}, device_id_type=MESH)
    pl.semaphore_wait(barrier, nb + nz)

    wide = jnp.broadcast_to(scale_ref[...], (LANE, LANE)).T
    for c in range(NC):
        spread[c] = wide[c * KC:(c + 1) * KC]

    def lanes(i):
        return pl.ds(pl.multiple_of(i * LB, LB), LB)

    def tiled(x):
        return jnp.concatenate([x] * (LB // LANE), axis=1)

    def two(x):
        return x.reshape(2, HB, x.shape[-1])

    def drift(c):
        load_noise(c).wait()
        sp = tiled(spread[c])

        def block(i, _):
            total = jnp.zeros((KC, LB), jnp.float32)
            for t in range(T):
                total = total + sp * noise[c, t, :, lanes(i)].astype(jnp.float32)
                work[c, t, :, lanes(i)] = total
            own[0, c, :, :, lanes(i)] = two(total)
            return 0

        lax.fori_loop(0, V // LB, block, 0)
        mate_copy(0, c).start()

    def first_hop(p, c):
        mate_copy(p, c).wait_recv()
        src[p, 0, c] = own[p, c, core] + mate[p, c, core]
        hop_copy(p, 0, c).start()

    def next_hop(p, j, c):
        hop_copy(p, j, c).wait_recv()
        arrived = got[p, j, c]
        wanted = bit(j + 1) == (1 - p)
        before = jnp.where(wanted, arrived, jnp.zeros_like(arrived))
        if j > 0:
            before = before + acc[p, c, core]
        acc[p, c, core] = before
        if j < nb - 1:
            src[p, j + 1, c] = src[p, j, c] + arrived
            hop_copy(p, j + 1, c).start()
            return
        acc_copy(p, c).start()
        if p == 1:
            @pl.when((me * rows) // KC == c)
            def _():
                tot[core] = src[p, j, c] + arrived

            @pl.when((partner * rows) // KC == c)
            def _():
                tot_out[...] = src[p, j, c] + arrived
                tot_copy().start()

    def entering(p, c, i):
        x = acc[p, c, :, :, lanes(i)].reshape(KC, LB)
        m = mate[p, c, :, :, lanes(i)].reshape(KC, LB)
        return x + jnp.where(core == 1 - p, m, jnp.zeros_like(m))

    def soft(c):
        acc_copy(0, c).wait_recv()
        load_base(c).wait()

        def seek(i, top):
            q = base[c, :, lanes(i)] + entering(0, c, i)
            query[:, lanes(i)] = q
            for b in range(LB // LANE):
                top = jnp.maximum(top, q[:, b * LANE:(b + 1) * LANE])
            return top

        top = lax.fori_loop(0, V // LB, seek, jnp.full((KC, LANE), -jnp.inf, jnp.float32))
        top = jnp.broadcast_to(jnp.max(top, axis=1, keepdims=True), (KC, LANE))
        tops = tiled(top)

        def block(i, sums):
            q = query[:, lanes(i)] - tops
            new = []
            for t in range(T):
                e = jnp.exp(work[c, t, :, lanes(i)] + q)
                work[c, t, :, lanes(i)] = e
                s = sums[t]
                for b in range(LB // LANE):
                    s = s + e[:, b * LANE:(b + 1) * LANE]
                new.append(s)
            return tuple(new)

        sums = lax.fori_loop(0, V // LB, block, tuple(jnp.zeros((KC, LANE), jnp.float32) for _ in range(T)))
        load_counts(c).wait()
        tokens = jnp.dot(counts[c].reshape(T * KC, V), jnp.ones((V, LANE), jnp.bfloat16),
                         preferred_element_type=jnp.float32)
        lane = lax.broadcasted_iota(jnp.int32, (KC, LANE), 1)
        packed = jnp.zeros((KC, LANE), jnp.float32)
        for t in range(T):
            s = jnp.broadcast_to(jnp.sum(sums[t], axis=1, keepdims=True), (KC, LANE))
            packed = jnp.where(lane == t, s, packed)
            packed = jnp.where(lane == T + t, tokens[t * KC:(t + 1) * KC], packed)
        stat[c, 0] = packed
        stat[c, 1] = top
        for d in range(1, nz):
            stat_copy(d, c).start()

    def slopes(c):
        for d in range(1, nz):
            stat_copy(d, c).wait_recv()
        mine, top = stat[c, 0], stat[c, 1]
        best = top
        for d in range(1, nz):
            best = jnp.maximum(best, stat_in[d - 1, c, 1])
        factor = jnp.exp(top - best)
        total = mine * factor
        tokens = mine
        for d in range(1, nz):
            total = total + stat_in[d - 1, c, 0] * jnp.exp(stat_in[d - 1, c, 1] - best)
            tokens = tokens + stat_in[d - 1, c, 0]
        r = factor * pltpu.roll(tokens, LANE - T, 1) / total
        for t in range(T):
            ratio[t] = jnp.broadcast_to(r[:, t:t + 1], (KC, LANE))
        sp = tiled(spread[c])

        def block(i, _):
            run = jnp.zeros((KC, LB), jnp.float32)
            for t in reversed(range(T)):
                run = run + (counts[c, t, :, lanes(i)].astype(jnp.float32)
                             - tiled(ratio[t]) * work[c, t, :, lanes(i)])
                work[c, t, :, lanes(i)] = sp * run - noise[c, t, :, lanes(i)].astype(jnp.float32)
            own[1, c, :, :, lanes(i)] = two(run)
            return 0

        lax.fori_loop(0, V // LB, block, 0)
        mate_copy(1, c).start()

    def finish(c):
        acc_copy(1, c).wait_recv()
        sp = tiled(spread[c])

        def block(i, _):
            later = sp * entering(1, c, i)
            for t in range(T):
                out[c, t, :, lanes(i)] = (work[c, t, :, lanes(i)] + later).astype(jnp.bfloat16)
            return 0

        lax.fori_loop(0, V // LB, block, 0)
        store_out(c).start()

    span = nb + 3
    forward = []
    for p in (0, 1):
        for j in reversed(range(nb)):
            forward.append((p * span + 2 + j, functools.partial(next_hop, p, j)))
        forward.append((p * span + 1, functools.partial(first_hop, p)))
    heavy = [(span, slopes), (nb + 2, soft), (0, drift), (span + nb + 2, finish)]

    def tick(s, _):
        for off, stage in forward + heavy:
            @pl.when((s >= off) & (s < off + NC))
            def _():
                stage(s - off)
        return 0

    lax.fori_loop(0, NC + span + nb + 2 + 1, tick, 0)


    tot_copy().wait()
    first = me * rows - ((me * rows) // KC) * KC
    if out_rows == KC:
        done = [pltpu.make_async_copy(tot.at[h], gb_hbm.at[pl.ds(h * HB, HB), :], gb_sem.at[h]) for h in range(2)]
    else:
        done = [pltpu.make_async_copy(tot.at[first // HB], gb_hbm, gb_sem.at[0])]
    for copy in done:
        copy.start()

    def drain(c, _):
        for p in (0, 1):
            mate_copy(p, c).wait_send()
            for j in range(nb):
                hop_copy(p, j, c).wait_send()
            acc_copy(p, c).wait_send()
        for d in range(1, nz):
            stat_copy(d, c).wait_send()
        store_out(c).wait()
        return 0

    lax.fori_loop(0, NC, drain, 0)
    for copy in done:
        copy.wait()


def per_device(n, nz, drift_noise, counts, base_logits, drift_scale):
    T, K, V = drift_noise.shape
    nb = n.bit_length() - 2
    rows = K // n
    out_rows = KC if rows >= KC else HB
    NC = K // KC
    f32, bf16 = jnp.float32, jnp.bfloat16
    dma = pltpu.SemaphoreType.DMA
    any_space = pl.BlockSpec(memory_space=pl.ANY)
    peers = max(nz - 1, 1)
    grad_noise, grad_base = pl.pallas_call(
        functools.partial(kernel, n, nz, nb, rows, out_rows, (T, K, V)),
        out_shape=(jax.ShapeDtypeStruct((T, K, V), bf16), jax.ShapeDtypeStruct((out_rows, V), f32)),
        in_specs=[any_space, any_space, any_space, pl.BlockSpec(memory_space=pltpu.VMEM)],
        out_specs=(any_space, any_space),
        scratch_shapes=[
            pltpu.VMEM((NC, T, KC, V), bf16),
            pltpu.VMEM((NC, T, KC, V), bf16),
            pltpu.VMEM((NC, KC, V), f32),
            pltpu.VMEM((NC, KC, LANE), f32),
            pltpu.VMEM((NC, T, KC, V), f32),
            pltpu.VMEM((NC, T, KC, V), bf16),
            pltpu.VMEM((KC, V), f32),
            pltpu.VMEM((T, KC, LANE), f32),
            pltpu.VMEM((NC, 2, KC, LANE), f32),
            pltpu.VMEM((peers, NC, 2, KC, LANE), f32),
            pltpu.VMEM((2, HB, V), f32),
            pltpu.VMEM((HB, V), f32),
            pltpu.VMEM((2, NC, 2, HB, V), f32),
            pltpu.VMEM((2, NC, 2, HB, V), f32),
            pltpu.VMEM((2, nb, NC, HB, V), f32),
            pltpu.VMEM((2, nb, NC, HB, V), f32),
            pltpu.VMEM((2, NC, 2, HB, V), f32),
            dma((3, NC)), dma((NC,)), dma((2,)),
            dma((2, NC)), dma((2, NC)),
            dma((2, nb, NC)), dma((2, nb, NC)),
            dma((2, NC)), dma((2, NC)),
            dma((peers, NC)), dma((peers, NC)),
            dma((1,)), dma((1,)),
        ],
        compiler_params=pltpu.CompilerParams(
            collective_id=0, has_side_effects=True, vmem_limit_bytes=60 * 1024 * 1024),
    )(drift_noise, counts, base_logits, drift_scale.reshape(1, K))
    if rows < out_rows:
        start = lax.rem(lax.axis_index("tm") * rows, out_rows)
        grad_base = lax.dynamic_slice_in_dim(grad_base, start, rows, 0)
    return grad_noise, grad_base


def solution(mesh):
    n, nz = mesh.shape["tm"], mesh.shape["vocab"]
    return jax.shard_map(
        functools.partial(per_device, n, nz),
        mesh=mesh,
        in_specs=(P("tm", None, "vocab"), P("tm", None, "vocab"), P(None, "vocab"), P()),
        out_specs=(P("tm", None, "vocab"), P("tm", "vocab")),
        check_vma=False,
    )
```

```python
import functools

import jax
import jax.numpy as jnp
from jax import lax
from jax.experimental import pallas as pl
from jax.experimental.pallas import tpu as pltpu
from jax.sharding import PartitionSpec as P

MESH = pl.DeviceIdType.MESH
KC = 16
HB = KC // 2
LANE = 128
GAP = (1, 3, 3)


def kernel(n, nz, nb, rows, out_rows, dims,
           noise_hbm, counts_hbm, base_hbm, scale_hbm, gn_hbm, gb_hbm,
           noise, counts, base, scale_ref, spread, work, out, query, ratio, stat, stat_in, tot, tot_out,
           own, mate, src, got, acc,
           in_sem, out_sem, gb_sem, scale_sem, mate_s, mate_r, hop_s, hop_r, acc_s, acc_r, stat_s, stat_r, tot_s, tot_r):
    T, K, V = dims
    NC = K // KC
    LB = min(256, V)
    me = lax.axis_index("tm")
    z = lax.axis_index("vocab")
    core = lax.rem(me, 2)
    partner = me + 1 - 2 * core

    def bit(j):
        return lax.rem(me // (2 ** j), 2)

    def across(j):
        return me + (1 - 2 * bit(j)) * (2 ** j)

    def krows(c):
        return pl.ds(pl.multiple_of(c * KC, KC), KC)

    def load_noise(c):
        return pltpu.make_async_copy(noise_hbm.at[:, krows(c), :], noise.at[c], in_sem.at[0, c])

    def load_counts(c):
        return pltpu.make_async_copy(counts_hbm.at[:, krows(c), :], counts.at[c], in_sem.at[1, c])

    def load_base(c):
        return pltpu.make_async_copy(base_hbm.at[krows(c), :], base.at[c], in_sem.at[2, c])

    def store_out(c):
        return pltpu.make_async_copy(out.at[c], gn_hbm.at[:, krows(c), :], out_sem.at[c])

    def send(a, b, s, r, device):
        return pltpu.make_async_remote_copy(src_ref=a, dst_ref=b, send_sem=s, recv_sem=r,
                                            device_id=device, device_id_type=MESH)

    def mate_copy(p, c):
        return send(own.at[p, c], mate.at[p, c], mate_s.at[p, c], mate_r.at[p, c], {"tm": partner})

    def hop_copy(p, j, c):
        return send(src.at[p, j, c], got.at[p, j, c], hop_s.at[p, j, c], hop_r.at[p, j, c],
                    {"tm": across(j + 1)})

    def acc_copy(p, c):
        return send(acc.at[p, c, core], acc.at[p, c, core], acc_s.at[p, c], acc_r.at[p, c], {"tm": partner})

    def stat_copy(d, c):
        return send(stat.at[c], stat_in.at[d - 1, c], stat_s.at[d - 1, c], stat_r.at[d - 1, c],
                    {"vocab": lax.rem(z + d, nz)})

    def tot_copy():
        return send(tot_out, tot.at[core], tot_s.at[0], tot_r.at[0], {"tm": partner})

    def start_loads(c, _):
        load_noise(c).start()
        load_base(c).start()
        return 0

    load_scale = pltpu.make_async_copy(scale_hbm, scale_ref, scale_sem.at[0])
    load_scale.start()
    lax.fori_loop(0, NC, start_loads, 0)
    lax.fori_loop(0, NC, lambda c, _: (load_counts(c).start(), 0)[1], 0)

    barrier = pltpu.get_barrier_semaphore()
    for j in range(nb + 1):
        pl.semaphore_signal(barrier, inc=1, device_id={"tm": across(j)}, device_id_type=MESH)
    for d in range(1, nz):
        pl.semaphore_signal(barrier, inc=1, device_id={"vocab": lax.rem(z + d, nz)}, device_id_type=MESH)
    pl.semaphore_wait(barrier, nb + nz)

    load_scale.wait()
    wide = jnp.broadcast_to(scale_ref[...], (LANE, LANE)).T
    for c in range(NC):
        spread[c] = wide[c * KC:(c + 1) * KC]

    def lanes(i):
        return pl.ds(pl.multiple_of(i * LB, LB), LB)

    def tiled(x):
        return jnp.concatenate([x] * (LB // LANE), axis=1)

    def two(x):
        return x.reshape(2, HB, x.shape[-1])

    def drift(c):
        load_noise(c).wait()
        sp = tiled(spread[c])

        def block(i, _):
            total = jnp.zeros((KC, LB), jnp.float32)
            for t in range(T):
                total = total + sp * noise[c, t, :, lanes(i)].astype(jnp.float32)
                work[c, t, :, lanes(i)] = total
            own[0, c, :, :, lanes(i)] = two(total)
            return 0

        lax.fori_loop(0, V // LB, block, 0)
        mate_copy(0, c).start()

    def first_hop(p, c):
        mate_copy(p, c).wait_recv()
        src[p, 0, c] = own[p, c, core] + mate[p, c, core]
        hop_copy(p, 0, c).start()

    def next_hop(p, j, c):
        hop_copy(p, j, c).wait_recv()
        arrived = got[p, j, c]
        wanted = bit(j + 1) == (1 - p)
        before = jnp.where(wanted, arrived, jnp.zeros_like(arrived))
        if j > 0:
            before = before + acc[p, c, core]
        acc[p, c, core] = before
        if j < nb - 1:
            src[p, j + 1, c] = src[p, j, c] + arrived
            hop_copy(p, j + 1, c).start()
            return
        acc_copy(p, c).start()
        if p == 1:
            @pl.when((me * rows) // KC == c)
            def _():
                tot[core] = src[p, j, c] + arrived

            @pl.when((partner * rows) // KC == c)
            def _():
                tot_out[...] = src[p, j, c] + arrived
                tot_copy().start()

    def entering(p, c, i):
        x = acc[p, c, :, :, lanes(i)].reshape(KC, LB)
        m = mate[p, c, :, :, lanes(i)].reshape(KC, LB)
        return x + jnp.where(core == 1 - p, m, jnp.zeros_like(m))

    def soft(c):
        acc_copy(0, c).wait_recv()
        load_base(c).wait()

        def seek(i, top):
            q = base[c, :, lanes(i)] + entering(0, c, i)
            query[:, lanes(i)] = q
            for b in range(LB // LANE):
                top = jnp.maximum(top, q[:, b * LANE:(b + 1) * LANE])
            return top

        top = lax.fori_loop(0, V // LB, seek, jnp.full((KC, LANE), -jnp.inf, jnp.float32))
        top = jnp.broadcast_to(jnp.max(top, axis=1, keepdims=True), (KC, LANE))
        tops = tiled(top)

        def block(i, sums):
            q = query[:, lanes(i)] - tops
            new = []
            for t in range(T):
                e = jnp.exp(work[c, t, :, lanes(i)] + q)
                work[c, t, :, lanes(i)] = e
                s = sums[t]
                for b in range(LB // LANE):
                    s = s + e[:, b * LANE:(b + 1) * LANE]
                new.append(s)
            return tuple(new)

        sums = lax.fori_loop(0, V // LB, block, tuple(jnp.zeros((KC, LANE), jnp.float32) for _ in range(T)))
        load_counts(c).wait()
        tokens = jnp.dot(counts[c].reshape(T * KC, V), jnp.ones((V, LANE), jnp.bfloat16),
                         preferred_element_type=jnp.float32)
        lane = lax.broadcasted_iota(jnp.int32, (KC, LANE), 1)
        packed = jnp.zeros((KC, LANE), jnp.float32)
        for t in range(T):
            s = jnp.broadcast_to(jnp.sum(sums[t], axis=1, keepdims=True), (KC, LANE))
            packed = jnp.where(lane == t, s, packed)
            packed = jnp.where(lane == T + t, tokens[t * KC:(t + 1) * KC], packed)
        stat[c, 0] = packed
        stat[c, 1] = top
        for d in range(1, nz):
            stat_copy(d, c).start()

    def slopes(c):
        for d in range(1, nz):
            stat_copy(d, c).wait_recv()
        mine, top = stat[c, 0], stat[c, 1]
        best = top
        for d in range(1, nz):
            best = jnp.maximum(best, stat_in[d - 1, c, 1])
        factor = jnp.exp(top - best)
        total = mine * factor
        tokens = mine
        for d in range(1, nz):
            total = total + stat_in[d - 1, c, 0] * jnp.exp(stat_in[d - 1, c, 1] - best)
            tokens = tokens + stat_in[d - 1, c, 0]
        r = factor * pltpu.roll(tokens, LANE - T, 1) / total
        for t in range(T):
            ratio[t] = jnp.broadcast_to(r[:, t:t + 1], (KC, LANE))
        sp = tiled(spread[c])

        def block(i, _):
            run = jnp.zeros((KC, LB), jnp.float32)
            for t in reversed(range(T)):
                run = run + (counts[c, t, :, lanes(i)].astype(jnp.float32)
                             - tiled(ratio[t]) * work[c, t, :, lanes(i)])
                work[c, t, :, lanes(i)] = sp * run - noise[c, t, :, lanes(i)].astype(jnp.float32)
            own[1, c, :, :, lanes(i)] = two(run)
            return 0

        lax.fori_loop(0, V // LB, block, 0)
        mate_copy(1, c).start()

    def finish(c):
        acc_copy(1, c).wait_recv()
        sp = tiled(spread[c])

        def block(i, _):
            later = sp * entering(1, c, i)
            for t in range(T):
                out[c, t, :, lanes(i)] = (work[c, t, :, lanes(i)] + later).astype(jnp.bfloat16)
            return 0

        lax.fori_loop(0, V // LB, block, 0)
        store_out(c).start()

    gap = GAP
    at, plan = 0, []
    for p in (0, 1):
        at += gap[0]
        stages = [(at, functools.partial(first_hop, p))]
        for j in range(nb):
            at += gap[1]
            stages.append((at, functools.partial(next_hop, p, j)))
        at += gap[0]
        plan = stages[::-1] + plan
        if p == 0:
            enter = at
            at += gap[2]
            leave = at
    heavy = [(leave, slopes), (enter, soft), (0, drift), (at, finish)]
    forward = plan

    def tick(s, _):
        for off, stage in forward + heavy:
            @pl.when((s >= off) & (s < off + NC))
            def _():
                stage(s - off)
        return 0

    lax.fori_loop(0, NC + at, tick, 0)


    tot_copy().wait()
    first = me * rows - ((me * rows) // KC) * KC
    if out_rows == KC:
        done = [pltpu.make_async_copy(tot.at[h], gb_hbm.at[pl.ds(h * HB, HB), :], gb_sem.at[h]) for h in range(2)]
    else:
        done = [pltpu.make_async_copy(tot.at[first // HB], gb_hbm, gb_sem.at[0])]
    for copy in done:
        copy.start()

    def drain(c, _):
        for p in (0, 1):
            mate_copy(p, c).wait_send()
            for j in range(nb):
                hop_copy(p, j, c).wait_send()
            acc_copy(p, c).wait_send()
        for d in range(1, nz):
            stat_copy(d, c).wait_send()
        store_out(c).wait()
        return 0

    lax.fori_loop(0, NC, drain, 0)
    for copy in done:
        copy.wait()


def per_device(n, nz, drift_noise, counts, base_logits, drift_scale):
    T, K, V = drift_noise.shape
    nb = n.bit_length() - 2
    rows = K // n
    out_rows = KC if rows >= KC else HB
    NC = K // KC
    f32, bf16 = jnp.float32, jnp.bfloat16
    dma = pltpu.SemaphoreType.DMA
    any_space = pl.BlockSpec(memory_space=pl.ANY)
    peers = max(nz - 1, 1)
    grad_noise, grad_base = pl.pallas_call(
        functools.partial(kernel, n, nz, nb, rows, out_rows, (T, K, V)),
        out_shape=(jax.ShapeDtypeStruct((T, K, V), bf16), jax.ShapeDtypeStruct((out_rows, V), f32)),
        in_specs=[any_space] * 4,
        out_specs=(any_space, any_space),
        scratch_shapes=[
            pltpu.VMEM((NC, T, KC, V), bf16),
            pltpu.VMEM((NC, T, KC, V), bf16),
            pltpu.VMEM((NC, KC, V), f32),
            pltpu.VMEM((1, K), f32),
            pltpu.VMEM((NC, KC, LANE), f32),
            pltpu.VMEM((NC, T, KC, V), f32),
            pltpu.VMEM((NC, T, KC, V), bf16),
            pltpu.VMEM((KC, V), f32),
            pltpu.VMEM((T, KC, LANE), f32),
            pltpu.VMEM((NC, 2, KC, LANE), f32),
            pltpu.VMEM((peers, NC, 2, KC, LANE), f32),
            pltpu.VMEM((2, HB, V), f32),
            pltpu.VMEM((HB, V), f32),
            pltpu.VMEM((2, NC, 2, HB, V), f32),
            pltpu.VMEM((2, NC, 2, HB, V), f32),
            pltpu.VMEM((2, nb, NC, HB, V), f32),
            pltpu.VMEM((2, nb, NC, HB, V), f32),
            pltpu.VMEM((2, NC, 2, HB, V), f32),
            dma((3, NC)), dma((NC,)), dma((2,)), dma((1,)),
            dma((2, NC)), dma((2, NC)),
            dma((2, nb, NC)), dma((2, nb, NC)),
            dma((2, NC)), dma((2, NC)),
            dma((peers, NC)), dma((peers, NC)),
            dma((1,)), dma((1,)),
        ],
        compiler_params=pltpu.CompilerParams(
            collective_id=0, has_side_effects=True, vmem_limit_bytes=40 * 1024 * 1024),
    )(*[pltpu.with_memory_space_constraint(x, pltpu.HBM) for x in (drift_noise, counts, base_logits, drift_scale.reshape(1, K))])
    if rows < out_rows:
        start = lax.rem(lax.axis_index("tm") * rows, out_rows)
        grad_base = lax.dynamic_slice_in_dim(grad_base, start, rows, 0)
    return grad_noise, grad_base


def solution(mesh):
    n, nz = mesh.shape["tm"], mesh.shape["vocab"]
    return jax.shard_map(
        functools.partial(per_device, n, nz),
        mesh=mesh,
        in_specs=(P("tm", None, "vocab"), P("tm", None, "vocab"), P(None, "vocab"), P()),
        out_specs=(P("tm", None, "vocab"), P("tm", "vocab")),
        check_vma=False,
    )
```
